32 devices in a mesh: row: 2 (over y), col: 16 (over z, x, core).
Axes of the slice: x: 2, y: 2, z: 4, core: 2. Of those that a mesh axis runs over, the one named last changes fastest.
Arguments:
- tiles: bfloat16 [2048, 128, 128], P(('row', 'col')), may hold values from -0.09375 to 0.09375
- tile_row: int32 [2048], P(('row', 'col')), may hold values from 0 to 63, as said below
- tile_col: int32 [2048], P(('row', 'col')), may hold values from 0 to 127, as said below
- live_tiles: int32 [32], P(('row', 'col')), may hold values from 1 to 64, as said below
- primal: float32 [16, 1024, 128], P('col', 'row'), may hold values from 0 to 1.5
- dual: float32 [2, 4096, 128], P('row', 'col'), may hold values from 0 to 1
- cost: float32 [16, 1024], P('col', 'row'), may hold values from 0.2 to 2
- upper: float32 [16, 1024], P('col', 'row'), may hold values from 0.3 to 1.5
- cap_flag: int32 [16, 1024], P('col', 'row'), may hold values 0 or 1
- demand: float32 [2, 4096, 128], P('row', 'col'), may hold values from -6 to 6
- eq_flag: int32 [2, 4096], P('row', 'col'), may hold values 0 or 1
Outputs:
- primal_out: float32 [16, 1024, 128], P('col', 'row')
- dual_out: float32 [2, 4096, 128], P('row', 'col')
The draws below stay inside these ranges and needn't reach their ends.
Inputs may be any that keep to these rules, and one draw needn't show every extreme that they name: `tile_row`: the tile in slot s lies on device d = s // 64; its block row lies in [(d // 16) * 32, (d // 16 + 1) * 32). Block coordinates may repeat. `tile_col`: the tile in slot s, on device d = s // 64, has its block column in [(d % 16) * 8, (d % 16 + 1) * 8). `live_tiles`: some device uses all 64 slots in every draw; the others use varying numbers of slots, from 1 to 64.
All inputs are finite; a program needn't handle non-finite values. No bound on the sum of `cap_flag` or of `eq_flag` on one device may be relied on, other than what follows from the above.
Results may differ from the reference program's by a relative error of at most 0.0024.
Values may be sent and summed in bfloat16 or wider, within the bound.
No kernel may reach another device: no remote copies, remote signals or barrier semaphores. Data moves between devices by JAX's collectives and lax.ppermute only.
A program may use at most 64 MiB of HBM per device.

```python
import math
import jax
import jax.numpy as jnp
from jax import lax

BLK = 128
S = 128
ITERS = 2
RB_DEV = 2
TILES_DEV = 64
ROW_GROUPS = 2
COL_GROUPS = 16
ROWB_GRP = 32
COLB_GRP = 8
ROW_BLOCKS = 64
COL_BLOCKS = 128
YW = 4096
XW = 1024
SLOTS = 2048


def draw_tile_row(key, part):
    slot_ids = jnp.arange(SLOTS, dtype=jnp.int32)
    device = slot_ids // TILES_DEV
    group = device // COL_GROUPS
    offset = jax.random.randint(jax.random.fold_in(key, 11), (SLOTS,), 0, ROWB_GRP, dtype=jnp.int32)
    return group * ROWB_GRP + offset


def draw_tile_col(key, part):
    slot_ids = jnp.arange(SLOTS, dtype=jnp.int32)
    device = slot_ids // TILES_DEV
    group = device % COL_GROUPS
    offset = jax.random.randint(jax.random.fold_in(key, 23), (SLOTS,), 0, COLB_GRP, dtype=jnp.int32)
    return group * COLB_GRP + offset


def draw_live_tiles(key, part):
    count = SLOTS // TILES_DEV
    level = jax.random.randint(jax.random.fold_in(key, 31), (count,), 1, 17, dtype=jnp.int32)
    loads = jnp.maximum(1, TILES_DEV * level * level // 256)
    full = jax.random.randint(jax.random.fold_in(key, 37), (), 0, count, dtype=jnp.int32)
    return jnp.where(jnp.arange(count, dtype=jnp.int32) == full, TILES_DEV, loads).astype(jnp.int32)


def place_ends(array, stream_key, low, high):
    index_at = [jax.random.randint(jax.random.fold_in(stream_key, axis), (), 0, length) for axis, length in enumerate(array.shape)]
    longest = array.shape.index(max(array.shape))
    beside = index_at[:longest] + [(index_at[longest] + 1) % array.shape[longest]] + index_at[longest + 1:]
    return array.at[tuple(index_at)].set(low).at[tuple(beside)].set(high)


def block_levels(rng, dims, cuts, least, largest):
    def one(axis_at, shards_of):
        steps = jax.random.uniform(jax.random.fold_in(jax.random.fold_in(rng, 6), axis_at), (shards_of,), jnp.float32, least / len(cuts), largest / len(cuts))
        return jnp.repeat(jnp.exp(steps), dims[axis_at] // shards_of).reshape((-1,) + (1,) * (len(dims) - axis_at - 1))

    factor_of = one(*cuts[0])
    for cut in cuts[1:]:
        factor_of = factor_of * one(*cut)
    return factor_of


def scatter_about(key, shape, deviation, reach, split=(), held_as=jnp.bfloat16):
    entries = deviation * jax.random.normal(key, shape, jnp.float32)
    if split:
        entries = entries * block_levels(key, shape, split, -0.22, 0.18)
    return jnp.clip(entries, -reach, reach).astype(held_as)


def setup_inputs(seed: int = 0) -> dict:
    keys = jax.random.split(jax.random.key(seed), 12)
    return {
        "tiles": scatter_about(keys[0], (SLOTS, BLK, BLK), (BLK * TILES_DEV // RB_DEV) ** -0.5, 0.09375, ((0, 32),)),
        "tile_row": draw_tile_row(jax.random.fold_in(keys[11], 71), 0),
        "tile_col": draw_tile_col(jax.random.fold_in(keys[11], 71), 0),
        "live_tiles": draw_live_tiles(jax.random.fold_in(keys[11], 71), 0),
        "primal": jnp.clip(1.5 * jax.random.uniform(keys[4], (COL_GROUPS, XW, S), jnp.float32) ** block_levels(keys[4], (COL_GROUPS, XW, S), ((0, 16), (1, 2)), -0.2, 0.2), 0.0, 1.5),
        "dual": jnp.clip(1.0 * jax.random.uniform(keys[5], (ROW_GROUPS, YW, S), jnp.float32) ** block_levels(keys[5], (ROW_GROUPS, YW, S), ((0, 2), (1, 16)), -0.2, 0.2), 0.0, 1.0),
        "cost": jnp.clip(jnp.exp(math.log(2.0) - 2.3025851 * jax.random.uniform(keys[6], (COL_GROUPS, XW), jnp.float32) ** block_levels(keys[6], (COL_GROUPS, XW), ((0, 16), (1, 2)), -0.2, 0.2)), 0.2, 2.0),
        "upper": jnp.clip(0.3 + 1.2 * jax.random.uniform(keys[7], (COL_GROUPS, XW), jnp.float32) ** block_levels(keys[7], (COL_GROUPS, XW), ((0, 16), (1, 2)), -0.2, 0.2), 0.3, 1.5),
        "cap_flag": place_ends((jax.random.randint(keys[8], (COL_GROUPS, XW), 0, 2) < 1).astype(jnp.int32), jax.random.fold_in(keys[8], 1), 0, 1),
        "demand": scatter_about(keys[9], (ROW_GROUPS, YW, S), 1.0, 6.0, ((0, 2), (1, 16)), jnp.float32),
        "eq_flag": place_ends((jax.random.randint(keys[10], (ROW_GROUPS, YW), 0, 4) < 1).astype(jnp.int32), jax.random.fold_in(keys[10], 1), 0, 1),
    }


tau_step = 0.4
sigma_step = 0.4


def reference(tiles, tile_row, tile_col, live_tiles, primal, dual, cost, upper, cap_flag, demand, eq_flag):
    groups = SLOTS // TILES_DEV
    slot_ids = jnp.arange(SLOTS, dtype=jnp.int32)
    live_rep = jnp.repeat(live_tiles, TILES_DEV)
    weights = ((slot_ids % TILES_DEV) < live_rep).astype(jnp.float32)
    tiles_c = tiles.reshape(groups, TILES_DEV, BLK, BLK)
    rows_c = tile_row.reshape(groups, TILES_DEV)
    cols_c = tile_col.reshape(groups, TILES_DEV)
    weight_c = weights.reshape(groups, TILES_DEV)

    def apply_forward(xb):
        def step(acc, item):
            tile, rows, cols, wgt = item
            picked = xb[cols].astype(jnp.float32)
            prod = jnp.einsum("kij,kjs->kis", tile.astype(jnp.float32), picked) * wgt[:, None, None]
            return acc.at[rows].add(prod), None
        start = jnp.zeros((ROW_BLOCKS, BLK, S), jnp.float32)
        return lax.scan(step, start, (tiles_c, rows_c, cols_c, weight_c))[0]

    def apply_transpose(yb):
        def step(acc, item):
            tile, rows, cols, wgt = item
            picked = yb[rows].astype(jnp.float32)
            prod = jnp.einsum("kij,kis->kjs", tile.astype(jnp.float32), picked) * wgt[:, None, None]
            return acc.at[cols].add(prod), None
        start = jnp.zeros((COL_BLOCKS, BLK, S), jnp.float32)
        return lax.scan(step, start, (tiles_c, rows_c, cols_c, weight_c))[0]

    x = primal.reshape(COL_BLOCKS, BLK, S)
    y = dual.reshape(ROW_BLOCKS, BLK, S)
    cost_b = cost.reshape(COL_BLOCKS, BLK, 1)
    bound = jnp.where(cap_flag == 1, upper, jnp.inf).reshape(COL_BLOCKS, BLK, 1)
    demand_b = demand.reshape(ROW_BLOCKS, BLK, S)
    equal = (eq_flag == 1).reshape(ROW_BLOCKS, BLK, 1)
    for step_index in range(ITERS):
        yb = y.astype(jnp.bfloat16)
        grad = apply_transpose(yb)
        x_new = jnp.minimum(jnp.maximum(x - tau_step * (cost_b - grad), 0.0), bound)
        xbar = (2.0 * x_new - x).astype(jnp.bfloat16)
        image = apply_forward(xbar)
        moved = y + sigma_step * (demand_b - image)
        y = jnp.where(equal, moved, jnp.maximum(moved, 0.0))
        x = x_new
    return x.reshape(primal.shape), y.reshape(dual.shape)
```

```python
import functools

import jax
import jax.numpy as jnp
from jax import lax
from jax.experimental import pallas as pl
from jax.experimental.pallas import tpu as pltpu
from jax.sharding import PartitionSpec as P

BLK = 128
ITERS = 2
UNROLL = 8


tau_step = 0.4
sigma_step = 0.4

VM = pl.BlockSpec(memory_space=pltpu.VMEM)
SM = pl.BlockSpec(memory_space=pltpu.SMEM)
bf16 = jnp.bfloat16
f32 = jnp.float32


def shape(dims, dtype):
    return jax.ShapeDtypeStruct(dims, dtype)


def apply_kernel(n_src, per, col_blocks, row_ref, col_ref, live_ref, tiles_ref, *refs):
    srcs = refs[:n_src]
    own_ref, send_ref, y_ref, acc_ref = refs[n_src:]
    for k in range(n_src):
        y_ref[k * per : (k + 1) * per] = srcs[k][...]
    acc_ref[...] = jnp.zeros_like(acc_ref)
    groups = (live_ref[0] + UNROLL - 1) // UNROLL

    def body(g, carry):
        base = g * UNROLL
        prods = []
        for u in range(UNROLL):
            t = base + u
            prods.append(
                jnp.dot(y_ref[row_ref[t]], tiles_ref[t], preferred_element_type=f32)
            )
        for u in range(UNROLL):
            acc_ref[col_ref[base + u]] += prods[u]
        return carry

    lax.fori_loop(0, groups, body, 0)
    total = acc_ref[:col_blocks]
    own_ref[...] = total
    send_ref[...] = total.astype(bf16)


def primal_kernel(
    n_recv, roll, col_blocks, row_blocks, keep, row_ref, col_ref, live_ref, tiles_ref,
    x_ref, cost_ref, bound_ref, own_ref, *refs
):
    recvs = refs[:n_recv]
    xn_ref, keep_ref, *rest = refs[n_recv:]
    xb_ref, acc_ref = rest[-2:]
    for b in range(col_blocks):
        grad = own_ref[b]
        for recv in recvs:
            grad = grad + recv[(b + roll) % col_blocks].astype(f32)
        x = x_ref[b]
        xn = jnp.minimum(jnp.maximum(x - tau_step * (cost_ref[b] - grad), 0.0), bound_ref[b])
        xn_ref[b] = xn
        xb_ref[b] = (2.0 * xn - x).astype(bf16)
    acc_ref[...] = jnp.zeros_like(acc_ref)
    groups = (live_ref[0] + UNROLL - 1) // UNROLL

    def body(g, carry):
        base = g * UNROLL
        prods = []
        for u in range(UNROLL):
            t = base + u
            prods.append(
                lax.dot_general(
                    xb_ref[col_ref[t]], tiles_ref[t], (((1,), (1,)), ((), ())),
                    preferred_element_type=f32,
                )
            )
        for u in range(UNROLL):
            acc_ref[row_ref[base + u]] += prods[u]
        return carry

    lax.fori_loop(0, groups, body, 0)
    keep_ref[...] = acc_ref[:keep]
    if keep < row_blocks:
        rest[0][...] = acc_ref[keep:row_blocks].astype(bf16)


def split_kernel(per, n_chips, *refs):
    n_in = len(refs) - n_chips
    ins, outs = refs[:n_in], refs[n_in:]
    for k in range(n_chips):
        part = ins[0][k * per : (k + 1) * per]
        for ref in ins[1:]:
            part = part + ref[k * per : (k + 1) * per].astype(f32)
        outs[k][...] = part.astype(outs[k].dtype)


def dual_kernel(last, n_recv, y_ref, demand_ref, equal_ref, own_ref, *refs):
    image = own_ref[...]
    for recv in refs[:n_recv]:
        image = image + recv[...].astype(f32)
    moved = y_ref[...] + sigma_step * (demand_ref[...] - image)
    y = jnp.where(equal_ref[...] == 1, moved, jnp.maximum(moved, 0.0))
    if last:
        for b in range(y.shape[0]):
            refs[n_recv][b * BLK : (b + 1) * BLK] = y[b].T
    else:
        refs[n_recv][...] = y
        refs[n_recv + 1][...] = y.astype(bf16)


def blocks_t(a):
    rows, scen = a.shape
    return a.reshape(rows // BLK, BLK, scen).transpose(0, 2, 1)


def per_device(
    tiles, tile_row, tile_col, live_tiles, primal, dual, cost, upper, cap_flag, demand, eq_flag
):
    n_tiles = tiles.shape[0]
    scen = primal.shape[2]
    n_col = lax.axis_size("col")
    n_row = lax.axis_size("row")
    r_per = dual.shape[1] // BLK
    c_per = primal.shape[1] // BLK
    row_blocks = r_per * n_col
    col_blocks = c_per * n_row
    cores = 2 if n_col % 2 == 0 else 1
    chips = n_col // cores
    xor = chips & (chips - 1) == 0
    pair = n_row == 2
    me_row = lax.axis_index("row")
    me_col = lax.axis_index("col")
    me_chip, me_core = me_col // cores, me_col % cores

    def to_chip(v, k):
        perm = []
        for c in range(n_col):
            chip, core = divmod(c, cores)
            other = chip ^ k if xor else (chip + k) % chips
            perm.append((c, other * cores + core))
        return lax.ppermute(v, "col", perm)

    def from_chip(v, k):
        return to_chip(v, k if xor else chips - k)

    def swap_core(v):
        return lax.ppermute(v, "col", [(c, c ^ 1) for c in range(n_col)])

    local_row = tile_row - me_row * row_blocks
    local_col = tile_col - me_col * col_blocks
    holder, sub = local_row // r_per, local_row % r_per
    chip, core = holder // cores, holder % cores
    away = chip ^ me_chip if xor else (chip - me_chip) % chips
    row_at = (((core - me_core) % cores) * chips + away) * r_per + sub
    col_at = (local_col - me_row * c_per) % col_blocks if pair else local_col
    alive = jnp.arange(n_tiles, dtype=jnp.int32) < live_tiles[0]
    row_in, col_in = row_at, col_at
    row_out = jnp.where(alive, row_at, row_blocks)
    col_out = jnp.where(alive, col_at, col_blocks)

    y = blocks_t(dual[0])
    yb = y.astype(bf16)
    demand_t = blocks_t(demand[0])
    equal = eq_flag.reshape(r_per, 1, BLK)
    bound = jnp.where(cap_flag == 1, upper, jnp.inf)
    lines = jnp.stack([cost, bound]).reshape(2, c_per, 1, BLK)
    x = blocks_t(primal[0])
    if pair:
        swap_row = lambda v: lax.ppermute(v, "row", [(0, 1), (1, 0)])
        x = jnp.concatenate([x, swap_row(x)], axis=0)
        lines = jnp.concatenate([lines, swap_row(lines)], axis=1)
    elif n_row > 1:
        x = lax.all_gather(x, "row", axis=0, tiled=True)
        lines = lax.all_gather(lines, "row", axis=1, tiled=True)
    cost_t, bound_t = lines[0], lines[1]

    keep = row_blocks // cores
    params = pltpu.CompilerParams(vmem_limit_bytes=24 * 1024 * 1024)
    for step_index in range(ITERS):
        last = step_index == ITERS - 1
        mine = [yb] + [from_chip(yb, k) for k in range(1, chips)]
        parts = mine + ([swap_core(v) for v in mine] if cores == 2 else [])
        n_src = len(parts)
        own, send = pl.pallas_call(
            functools.partial(apply_kernel, n_src, r_per, col_blocks),
            out_shape=(
                shape((col_blocks, scen, BLK), f32),
                shape((col_blocks, scen, BLK), bf16),
            ),
            in_specs=[SM, SM, SM] + [VM] * (1 + n_src),
            out_specs=(VM, VM),
            scratch_shapes=[
                pltpu.VMEM((row_blocks, scen, BLK), bf16),
                pltpu.VMEM((col_blocks + 1, scen, BLK), f32),
            ],
            compiler_params=params,
            name="apply_rows",
        )(row_in, col_out, live_tiles, tiles, *parts)
        if pair:
            recvs = [swap_row(send)]
        else:
            recvs = []
            own = lax.psum(own, "row")
        n_recv = len(recvs)
        outs = pl.pallas_call(
            functools.partial(primal_kernel, n_recv, c_per, col_blocks, row_blocks, keep),
            out_shape=[
                shape((col_blocks, scen, BLK), f32),
                shape((keep, scen, BLK), f32),
            ] + ([shape((row_blocks - keep, scen, BLK), bf16)] if cores == 2 else []),
            in_specs=[SM, SM, SM] + [VM] * (5 + n_recv),
            out_specs=[VM] * (1 + cores),
            scratch_shapes=[
                pltpu.VMEM((col_blocks, scen, BLK), bf16),
                pltpu.VMEM((row_blocks + 1, scen, BLK), f32),
            ],
            compiler_params=params,
            name="apply_cols",
        )(row_out, col_in, live_tiles, tiles, x, cost_t, bound_t, own, *recvs)
        x = outs[0]
        sums = [outs[1]] + ([swap_core(outs[2])] if cores == 2 else [])
        pieces = pl.pallas_call(
            functools.partial(split_kernel, r_per, chips),
            out_shape=[shape((r_per, scen, BLK), f32 if k == 0 else bf16) for k in range(chips)],
            in_specs=[VM] * len(sums),
            out_specs=[VM] * chips,
            compiler_params=params,
            name="split_rows",
        )(*sums)
        arrived = [to_chip(pieces[k], k) for k in range(1, chips)]
        if last:
            dual_shape = [shape(dual.shape[1:], f32)]
        else:
            dual_shape = [shape(y.shape, f32), shape(y.shape, bf16)]
        res = pl.pallas_call(
            functools.partial(dual_kernel, last, chips - 1),
            out_shape=dual_shape,
            in_specs=[VM] * (3 + chips),
            out_specs=[VM] * len(dual_shape),
            compiler_params=params,
            name="dual_step",
        )(y, demand_t, equal, pieces[0], *arrived)
        if last:
            y = res[0]
        else:
            y, yb = res
    if pair:
        x = x[:c_per]
    else:
        x = lax.dynamic_slice_in_dim(x, me_row * c_per, c_per, axis=0)
    x = x.transpose(0, 2, 1).reshape(primal.shape)
    return (x, y.reshape(dual.shape))


def solution(mesh):
    return jax.shard_map(
        per_device,
        mesh=mesh,
        in_specs=(
            P(("row", "col"), None, None),
            P(("row", "col")),
            P(("row", "col")),
            P(("row", "col")),
            P("col", "row", None),
            P("row", "col", None),
            P("col", "row"),
            P("col", "row"),
            P("col", "row"),
            P("row", "col", None),
            P("row", "col"),
        ),
        out_specs=(P("col", "row", None), P("row", "col", None)),
        check_vma=False,
    )
```
